512 devices in a mesh: dp: 64 (over z_lo, x, core), mp: 8 (over z_hi, y).
Axes of the slice: x: 4, y: 4, z: 16 (z_hi: 2, z_lo: 8; z = z_hi * 8 + z_lo), core: 2. Of those that a mesh axis runs over, the one named last changes fastest.
Arguments:
- inputs: bfloat16 [1024, 6144], P('dp', 'mp'), may hold values from -6 to 6
- targets: bfloat16 [1024, 6144], P('dp', 'mp'), may hold values from -6 to 6
- w_in: bfloat16 [6144, 16384], P('mp', 'dp'), may hold values from -6 to 6
- w_out: bfloat16 [16384, 6144], P('dp', 'mp'), may hold values from -6 to 6
- teach_in: float32 [6144, 16384], P('mp', 'dp'), may hold values from -6 to 6
- teach_out: float32 [16384, 6144], P('dp', 'mp'), may hold values from -6 to 6
Outputs:
- grad_in: bfloat16 [6144, 16384], P('mp', 'dp')
- grad_out: bfloat16 [16384, 6144], P('dp', 'mp')
- new_in: float32 [6144, 16384], P('mp', 'dp')
- new_out: float32 [16384, 6144], P('dp', 'mp')
The draws below stay inside these ranges and needn't reach their ends.
All inputs are finite; a program needn't handle non-finite values.
Results may differ from the reference program's by a relative error of at most 0.017.
Values may be sent and summed in bfloat16 or wider, within the bound.
No kernel may reach another device: no remote copies, remote signals or barrier semaphores. Data moves between devices by JAX's collectives and lax.ppermute only.
A program may use at most 64 MiB of HBM per device.

```python
import math
import jax
import jax.numpy as jnp

D = 6144
FF = 16384
TOKENS = 1024


def block_levels(own_key, dims, shards, smallest, high):
    factor_of, own = 1.0, jax.random.fold_in(own_key, 6)
    for dim, blocks in shards:
        heights = jnp.exp(jax.random.uniform(jax.random.fold_in(own, dim), (blocks,), jnp.float32, smallest / len(shards), high / len(shards)))
        factor_of = factor_of * jnp.repeat(heights, dims[dim] // blocks).reshape([-1 if axis == dim else 1 for axis in range(len(dims))])
    return factor_of


def normal_values(key, dims, deviation, reach, shards=(), kind=jnp.bfloat16):
    values = jax.random.normal(key, dims, jnp.float32) * deviation
    if len(shards) > 0:
        values = block_levels(key, dims, shards, -0.22, 0.18) * values
    return jnp.clip(values, min=-reach, max=reach).astype(kind)


def setup_inputs(seed: int = 0) -> dict:
    arg_keys = jax.random.split(jax.random.key(seed), 7)
    inputs = normal_values(arg_keys[0], (TOKENS, D), 1.0, 6.0, ((0, 64), (1, 8)))
    targets = normal_values(arg_keys[1], (TOKENS, D), 1.0, 6.0, ((0, 64), (1, 8)))
    w_in = normal_values(arg_keys[2], (D, FF), 1.0, 6.0, ((0, 8), (1, 64)))
    w_out = normal_values(arg_keys[3], (FF, D), 1.0, 6.0, ((0, 64), (1, 8)))
    teach_in = normal_values(arg_keys[4], (D, FF), 1.0, 6.0, ((0, 8), (1, 64)), jnp.float32)
    teach_out = normal_values(arg_keys[5], (FF, D), 1.0, 6.0, ((0, 64), (1, 8)), jnp.float32)
    return dict(inputs=inputs, targets=targets, w_in=w_in, w_out=w_out, teach_in=teach_in, teach_out=teach_out)


decay_rate = 0.99
step_size = 0.5

def gelu_value(value):
    return 0.5 * value * (1.0 + jax.scipy.special.erf(value * (1.0 / math.sqrt(2.0))))

def gelu_slope(value):
    normal_cdf = 0.5 * (1.0 + jax.scipy.special.erf(value * (1.0 / math.sqrt(2.0))))
    return normal_cdf + value * jnp.exp(-0.5 * value * value) * (1.0 / math.sqrt(2.0 * math.pi))

def reference(inputs, targets, w_in, w_out, teach_in, teach_out):
    in_scale = 1.0 / math.sqrt(D)
    out_scale = 1.0 / math.sqrt(FF)
    preact = jnp.dot(inputs, w_in, preferred_element_type=jnp.float32) * in_scale
    hidden = gelu_value(preact).astype(jnp.bfloat16)
    outputs = inputs.astype(jnp.float32) + jnp.dot(hidden, w_out, preferred_element_type=jnp.float32) * out_scale
    slope = (outputs - targets.astype(jnp.float32)).astype(jnp.bfloat16)
    grad_out = jnp.dot(hidden.T, slope, preferred_element_type=jnp.float32) * out_scale
    hidden_slope = jnp.dot(slope, w_out.T, preferred_element_type=jnp.float32) * out_scale
    pre_slope = (hidden_slope * gelu_slope(preact)).astype(jnp.bfloat16)
    grad_in = jnp.dot(inputs.T, pre_slope, preferred_element_type=jnp.float32) * in_scale
    new_in = decay_rate * teach_in + (1.0 - decay_rate) * (w_in.astype(jnp.float32) - step_size * grad_in)
    new_out = decay_rate * teach_out + (1.0 - decay_rate) * (w_out.astype(jnp.float32) - step_size * grad_out)
    return (grad_in.astype(jnp.bfloat16), grad_out.astype(jnp.bfloat16), new_in, new_out)
```

```python
import math

import jax
import jax.numpy as jnp
from jax import lax
from jax.sharding import Mesh
from jax.sharding import PartitionSpec as P

D = 6144
FF = 16384
DP = ("zl", "x", "c")
MP = ("zh", "y")
BF = jnp.bfloat16
F32 = jnp.float32

decay_rate = 0.99
step_size = 0.5


def exchange(pieces, axis):
    return lax.all_to_all(pieces, axis, split_axis=0, concat_axis=0, tiled=True)


def gather(value, axis):
    return exchange(jnp.broadcast_to(value, (lax.axis_size(axis), *value.shape)), axis)


def gather_tokens(value):
    return gather(gather(gather(value, "zl"), "x"), "c")


def sum_pieces(pieces):
    return pieces.astype(F32).sum(axis=0)


def scatter_tokens(partial):
    own = sum_pieces(exchange(partial.astype(BF), "c"))
    own = sum_pieces(exchange(own.astype(BF), "x"))
    return sum_pieces(exchange(own.astype(BF), "zl"))


def gelu_value(value):
    return 0.5 * value * (1.0 + jax.scipy.special.erf(value * (1.0 / math.sqrt(2.0))))


def gelu_slope(value):
    normal_cdf = 0.5 * (1.0 + jax.scipy.special.erf(value * (1.0 / math.sqrt(2.0))))
    return normal_cdf + value * jnp.exp(-0.5 * value * value) * (1.0 / math.sqrt(2.0 * math.pi))


def shards(inputs, targets, w_in, w_out, teach_in, teach_out):
    in_scale = 1.0 / math.sqrt(D)
    out_scale = 1.0 / math.sqrt(FF)
    rows, d = inputs.shape
    f = w_in.shape[1]
    dims = tuple(lax.axis_size(a) for a in ("c", "x", "zl"))
    tokens = rows * math.prod(dims)
    groups = lax.axis_size("zh") * lax.axis_size("y")

    gathered = gather_tokens(inputs).reshape(tokens, d)
    partial_pre = jnp.dot(gathered, w_in, preferred_element_type=F32) * in_scale
    preact = sum_pieces(exchange(partial_pre.astype(BF).reshape(groups, tokens // groups, f), MP))
    hidden = gather(gelu_value(preact).astype(BF), MP).reshape(tokens, f)

    partial_out = jnp.dot(hidden, w_out, preferred_element_type=F32) * out_scale
    summed_rows = scatter_tokens(partial_out.reshape(*dims, rows, d))
    slope = (inputs.astype(F32) + summed_rows - targets.astype(F32)).astype(BF)
    slopes = gather_tokens(slope).reshape(tokens, d)

    slope_part = jnp.einsum("td,fd->tf", slopes, w_out, preferred_element_type=F32) * out_scale
    hidden_slope = sum_pieces(
        exchange(slope_part.astype(BF).reshape(groups, tokens // groups, f), MP)
    )
    pre_slope = (hidden_slope * gelu_slope(preact)).astype(BF)
    pre_slopes = gather(pre_slope, MP).reshape(tokens, f)

    grad_out = jnp.einsum("tf,td->fd", hidden, slopes, preferred_element_type=F32) * out_scale
    new_out = decay_rate * teach_out + (1.0 - decay_rate) * (
        w_out.astype(F32) - step_size * grad_out
    )
    grad_in = jnp.einsum("td,tf->df", gathered, pre_slopes, preferred_element_type=F32) * in_scale
    new_in = decay_rate * teach_in + (1.0 - decay_rate) * (w_in.astype(F32) - step_size * grad_in)
    return (grad_in.astype(BF), grad_out.astype(BF), new_in, new_out)


def solution(mesh):
    finer = Mesh(mesh.devices.reshape(8, 4, 2, 2, 4), ("zl", "x", "c", "zh", "y"))
    return jax.shard_map(
        shards,
        mesh=finer,
        in_specs=(P(DP, MP), P(DP, MP), P(MP, DP), P(DP, MP), P(MP, DP), P(DP, MP)),
        out_specs=(P(MP, DP), P(DP, MP), P(MP, DP), P(DP, MP)),
        check_vma=False,
    )
```

```python
import math

import jax
import jax.numpy as jnp
from jax import lax
from jax.sharding import Mesh
from jax.sharding import PartitionSpec as P

D = 6144
FF = 16384
DP = ("zq", "za", "x", "c")
MP = ("zh", "y")
BF = jnp.bfloat16
F32 = jnp.float32

decay_rate = 0.99
step_size = 0.5


def exchange(pieces, axis):
    return lax.all_to_all(pieces, axis, split_axis=0, concat_axis=0, tiled=True)


def gather(value, axis):
    return exchange(jnp.broadcast_to(value, (lax.axis_size(axis), *value.shape)), axis)


def scatter(partial, axis):
    return exchange(partial.astype(BF), axis).astype(F32).sum(axis=0)


def swap(value, axis):
    return lax.ppermute(value, axis, [(0, 1), (1, 0)])


def sum_pair(value, axis):
    return value + swap(value.astype(BF), axis).astype(F32)


def gelu_value(value):
    return 0.5 * value * (1.0 + jax.scipy.special.erf(value * (1.0 / math.sqrt(2.0))))


def gelu_slope(value):
    normal_cdf = 0.5 * (1.0 + jax.scipy.special.erf(value * (1.0 / math.sqrt(2.0))))
    return normal_cdf + value * jnp.exp(-0.5 * value * value) * (1.0 / math.sqrt(2.0 * math.pi))


def ema(teacher, student, grad):
    return decay_rate * teacher + (1.0 - decay_rate) * (student.astype(F32) - step_size * grad)


def shards(inputs, targets, w_in, w_out, teach_in, teach_out):
    in_scale = 1.0 / math.sqrt(D)
    out_scale = 1.0 / math.sqrt(FF)
    rows, d = inputs.shape
    f = w_in.shape[1]
    nx, na, nq, ny = (lax.axis_size(a) for a in ("x", "za", "zq", "y"))
    tokens = nx * na * nq * rows

    w_in2 = jnp.concatenate([w_in, swap(w_in, "c")], axis=1)
    w_out2 = jnp.concatenate([w_out, swap(w_out, "c")], axis=0)

    gathered = gather(gather(inputs, ("za", "zq")), "x").reshape(tokens, d)
    partial_pre = jnp.dot(gathered, w_in2, preferred_element_type=F32) * in_scale
    preact = sum_pair(scatter(partial_pre.reshape(ny, tokens // ny, 2 * f), "y"), "zh")
    hidden = gather(gelu_value(preact).astype(BF), "y").reshape(tokens, 2 * f)

    partial_out = jnp.dot(hidden, w_out2, preferred_element_type=F32) * out_scale
    sums = scatter(partial_out.reshape(nx, na * nq * rows, d), "x")
    sums = scatter(sums.reshape(na, nq, rows, d), "za")
    own = inputs.astype(F32) - targets.astype(F32)
    mine = lax.broadcasted_iota(jnp.int32, (nq, 1, 1), 0) == lax.axis_index("zq")
    slope = sum_pair(sums + jnp.where(mine, own[None], 0.0), "zq").astype(BF)
    slopes = gather(gather(slope, "za"), "x").reshape(tokens, d)

    slope_part = (
        jnp.einsum("td,fd->tf", slopes, w_out2, preferred_element_type=F32) * out_scale
    )
    hidden_slope = sum_pair(scatter(slope_part.reshape(ny, tokens // ny, 2 * f), "y"), "zh")
    pre_slope = (hidden_slope * gelu_slope(preact)).astype(BF)
    pre_slopes = gather(pre_slope, "y").reshape(tokens, 2 * f)

    part_out = jnp.einsum("tf,td->fd", hidden, slopes, preferred_element_type=F32) * out_scale
    grad_out = part_out[:f] + swap(part_out[f:].astype(BF), "c").astype(F32)
    new_out = ema(teach_out, w_out, grad_out)

    part_in = jnp.einsum("td,tf->df", gathered, pre_slopes, preferred_element_type=F32) * in_scale
    grad_in = part_in[:, :f] + swap(part_in[:, f:].astype(BF), "c").astype(F32)
    new_in = ema(teach_in, w_in, grad_in)
    return (grad_in.astype(BF), grad_out.astype(BF), new_in, new_out)


def solution(mesh):
    finer = Mesh(mesh.devices.reshape(2, 4, 4, 2, 2, 4), (*DP, *MP))
    return jax.shard_map(
        shards,
        mesh=finer,
        in_specs=(P(DP, MP), P(DP, MP), P(MP, DP), P(DP, MP), P(MP, DP), P(DP, MP)),
        out_specs=(P(MP, DP), P(DP, MP), P(MP, DP), P(DP, MP)),
        check_vma=False,
    )
```

```python
import math

import jax
import jax.numpy as jnp
from jax import lax
from jax.sharding import Mesh
from jax.sharding import PartitionSpec as P

D = 6144
FF = 16384
DP = ("zq", "za", "x", "c")
MP = ("zh", "y")
BF = jnp.bfloat16
F32 = jnp.float32

decay_rate = 0.99
step_size = 0.5


def exchange(pieces, axis):
    return lax.all_to_all(pieces, axis, split_axis=0, concat_axis=0, tiled=True)


def gather(value, axis):
    return exchange(jnp.broadcast_to(value, (lax.axis_size(axis), *value.shape)), axis)


def scatter(partial, axis):
    return exchange(partial.astype(BF), axis).astype(F32).sum(axis=0)


def shift(value, axis, by):
    n = lax.axis_size(axis)
    return lax.ppermute(value, axis, [(i, (i + by) % n) for i in range(n)])


def sum_pair(value, axis):
    return value + shift(value.astype(BF), axis, 1).astype(F32)


def gelu_value(value):
    return 0.5 * value * (1.0 + jax.scipy.special.erf(value * (1.0 / math.sqrt(2.0))))


def gelu_slope(value):
    normal_cdf = 0.5 * (1.0 + jax.scipy.special.erf(value * (1.0 / math.sqrt(2.0))))
    return normal_cdf + value * jnp.exp(-0.5 * value * value) * (1.0 / math.sqrt(2.0 * math.pi))


def ema(teacher, student, grad):
    return decay_rate * teacher + (1.0 - decay_rate) * (student.astype(F32) - step_size * grad)


def dot(a, b):
    return jnp.dot(a, b, preferred_element_type=F32)


def shards(inputs, targets, w_in, w_out, teach_in, teach_out):
    in_scale = 1.0 / math.sqrt(D)
    out_scale = 1.0 / math.sqrt(FF)
    rows, d = inputs.shape
    f = w_in.shape[1]
    nx, na, nq, ny = (lax.axis_size(a) for a in ("x", "za", "zq", "y"))
    blocks = nx * na * nq
    tokens = blocks * rows
    part = tokens // ny
    few = rows // ny
    y = lax.axis_index("y")

    w_in2 = jnp.concatenate([w_in, shift(w_in, "c", 1)], axis=1)
    w_ring = jnp.concatenate([w_out, *(shift(w_out, "y", -k) for k in range(1, ny))], axis=1)
    w_out2 = jnp.concatenate([w_ring, shift(w_ring, "c", 1)], axis=0)

    arrived = gather(gather(inputs, ("za", "zq")), "x").reshape(tokens, d)
    at = lax.broadcasted_iota(jnp.int32, (tokens, tokens), 0)
    here = at // part
    source = (at % part) // few * rows + here * few + at % few
    order = (source == lax.broadcasted_iota(jnp.int32, (tokens, tokens), 1)).astype(BF)
    gathered = dot(order, arrived).astype(BF)
    gathered_t = lax.optimization_barrier(gathered.T)

    partial_pre = dot(gathered, w_in2) * in_scale
    sums = scatter(partial_pre.reshape(ny, part, 2 * f), "y")

    both = jnp.stack([inputs.reshape(ny, few, d), targets.reshape(ny, few, d)], axis=1)
    both, sums = lax.optimization_barrier((both, sums))
    both = exchange(both, "y").astype(F32)
    own = both[:, 0] - both[:, 1]
    own = jnp.concatenate(
        [lax.dynamic_index_in_dim(own, (y + k) & (ny - 1), keepdims=False) for k in range(ny)],
        axis=1,
    )
    own, other = lax.optimization_barrier((own, shift(sums.astype(BF), "zh", 1)))
    preact = sums + other.astype(F32)
    hidden = gelu_value(preact).astype(BF)

    partial_out = dot(hidden, w_out2) * out_scale
    sums = scatter(partial_out.reshape(nx, part // nx, ny * d), "x")
    sums = scatter(sums.reshape(na, nq * few, ny * d), "za")
    mine = lax.broadcasted_iota(jnp.int32, (nq * few, 1), 0) // few == lax.axis_index("zq")
    sums = sums + jnp.where(mine, jnp.concatenate([own] * nq, axis=0), 0.0)
    slope = sum_pair(sums, "zq").astype(BF)
    slopes = gather(gather(slope, "za"), "x").reshape(part, ny * d)

    slope_part = jnp.einsum("td,fd->tf", slopes, w_out2, preferred_element_type=F32) * out_scale
    hidden_slope = sum_pair(slope_part, "zh")
    pre_slope = (hidden_slope * gelu_slope(preact)).astype(BF)
    pre_slopes = gather(pre_slope, "y").reshape(tokens, 2 * f)

    hiddens = jnp.concatenate([hidden, *(shift(hidden, "y", k) for k in range(1, ny))], axis=0)
    own_slopes = jnp.concatenate(
        [slopes[:, :d], *(shift(slopes[:, k * d : (k + 1) * d], "y", k) for k in range(1, ny))],
        axis=0,
    )

    def grad_of(units):
        return jnp.einsum("tf,td->fd", units, own_slopes, preferred_element_type=F32) * out_scale

    theirs = shift(grad_of(hiddens[:, f:]).astype(BF), "c", 1).astype(F32)
    grad_out = grad_of(hiddens[:, :f]) + theirs
    new_out = ema(teach_out, w_out, grad_out)

    theirs = shift((dot(gathered_t, pre_slopes[:, f:]) * in_scale).astype(BF), "c", 1).astype(F32)
    grad_in = dot(gathered_t, pre_slopes[:, :f]) * in_scale + theirs
    new_in = ema(teach_in, w_in, grad_in)
    return (grad_in.astype(BF), grad_out.astype(BF), new_in, new_out)


def solution(mesh):
    finer = Mesh(mesh.devices.reshape(2, 4, 4, 2, 2, 4), (*DP, *MP))
    return jax.shard_map(
        shards,
        mesh=finer,
        in_specs=(P(DP, MP), P(DP, MP), P(MP, DP), P(DP, MP), P(MP, DP), P(DP, MP)),
        out_specs=(P(MP, DP), P(DP, MP), P(MP, DP), P(DP, MP)),
        check_vma=False,
    )
```

```python
import math

import jax
import jax.numpy as jnp
import numpy as np
from jax import lax
from jax.experimental.layout import Layout, with_layout_constraint
from jax.sharding import Mesh
from jax.sharding import PartitionSpec as P

D = 6144
FF = 16384
DP = ("zq", "za", "x", "c")
MP = ("zh", "y")
BF = jnp.bfloat16
F32 = jnp.float32

decay_rate = 0.99
step_size = 0.5


def exchange(pieces, axis):
    return lax.all_to_all(pieces, axis, split_axis=0, concat_axis=0, tiled=True)


def gather(value, axis):
    return exchange(jnp.broadcast_to(value, (lax.axis_size(axis), *value.shape)), axis)


def scatter(partial, axis):
    return exchange(partial.astype(BF), axis).astype(F32).sum(axis=0)


def shift(value, axis, by):
    n = lax.axis_size(axis)
    return lax.ppermute(value, axis, [(i, (i + by) % n) for i in range(n)])


def gelu_value(value):
    return 0.5 * value * (1.0 + jax.scipy.special.erf(value * (1.0 / math.sqrt(2.0))))


def gelu_slope(value):
    normal_cdf = 0.5 * (1.0 + jax.scipy.special.erf(value * (1.0 / math.sqrt(2.0))))
    return normal_cdf + value * jnp.exp(-0.5 * value * value) * (1.0 / math.sqrt(2.0 * math.pi))


def ema(teacher, student, grad):
    return decay_rate * teacher + (1.0 - decay_rate) * (student.astype(F32) - step_size * grad)


def tie(*values):
    return lax.optimization_barrier(values)


def dot(a, b):
    return jnp.dot(a, b, preferred_element_type=F32)


def shards(inputs, targets, w_in, w_out, teach_in, teach_out):
    in_scale = 1.0 / math.sqrt(D)
    out_scale = 1.0 / math.sqrt(FF)
    rows, d = inputs.shape
    f = w_in.shape[1]
    nx, na, nq, ny = (lax.axis_size(a) for a in ("x", "za", "zq", "y"))
    blocks = nx * na * nq
    tokens = blocks * rows
    part = tokens // ny
    few = rows // ny
    y = lax.axis_index("y")

    w_both = shift(w_in, "c", 1)
    w_ring = [w_out, shift(w_out, "y", -1), None, shift(w_out, "y", 1)]
    near = gather(inputs, ("za", "zq"))
    near, w_both, w_ring[1], w_ring[3], w_later = tie(near, w_both, w_ring[1], w_ring[3], w_out)
    w_ring[2] = shift(w_later, "y", 2)
    w_both = jnp.concatenate([w_in, w_both], axis=1)

    arrived = gather(near, "x").reshape(tokens, d)
    arrived, w_both, *w_ring[1:] = tie(arrived, w_both, *w_ring[1:])
    at = np.arange(tokens)
    source = (at % part) // few * rows + at // part * few + at % few
    order = jnp.asarray(np.eye(tokens, dtype=np.float32)[source], BF)
    gathered = with_layout_constraint(dot(order, arrived).astype(BF), Layout((0, 1)))
    w_ring = jnp.concatenate(w_ring, axis=1)

    partial_pre = dot(gathered, w_both) * in_scale
    sums = scatter(partial_pre.reshape(ny, part, 2 * f), "y")

    sums, w_ring, arrived = tie(sums, w_ring, arrived)
    other = shift(sums.astype(BF), "zh", 1)
    w_ring_theirs = shift(w_ring, "c", 1)
    gathered_t = jnp.einsum("td,pt->dp", arrived, order, preferred_element_type=F32).astype(BF)

    both = jnp.stack([inputs.reshape(ny, few, d), targets.reshape(ny, few, d)], axis=1)
    both = exchange(both, "y")
    both = both.astype(F32)
    own = both[:, 0] - both[:, 1]
    own = jnp.concatenate(
        [lax.dynamic_index_in_dim(own, (y + k) & (ny - 1), keepdims=False) for k in range(ny)],
        axis=1,
    )
    own, other, gathered_t = tie(own, other, gathered_t)
    preact = sums + other.astype(F32)
    hidden = gelu_value(preact).astype(BF)
    hiddens = [shift(hidden, "y", k) for k in range(1, ny)]

    partial_out = (dot(hidden[:, :f], w_ring) + dot(hidden[:, f:], w_ring_theirs)) * out_scale
    sums = scatter(partial_out.reshape(nx, part // nx, ny * d), "x")
    sums, hiddens[0] = tie(sums, hiddens[0])
    sums = scatter(sums.reshape(na, nq * few, ny * d), "za")
    sums, hiddens[1] = tie(sums, hiddens[1])
    mine = lax.broadcasted_iota(jnp.int32, (nq * few, 1), 0) // few == lax.axis_index("zq")
    sums = sums + jnp.where(mine, jnp.concatenate([own] * nq, axis=0), 0.0)
    other = shift(sums.astype(BF), "zq", 1)
    other, hiddens[2] = tie(other, hiddens[2])
    slope = (sums + other.astype(F32)).astype(BF)
    slopes = gather(gather(slope, "za"), "x").reshape(part, ny * d)

    slope_part = out_scale * jnp.concatenate(
        [
            jnp.einsum("td,fd->tf", slopes, w, preferred_element_type=F32)
            for w in (w_ring, w_ring_theirs)
        ],
        axis=1,
    )
    slopes, slope_part = tie(slopes, slope_part)
    other = shift(slope_part.astype(BF), "zh", 1)
    their_slopes = [shift(slopes[:, k * d : (k + 1) * d], "y", k) for k in range(1, ny)]
    other, *their_slopes = tie(other, *their_slopes)
    hidden_slope = slope_part + other.astype(F32)
    pre_slope = (hidden_slope * gelu_slope(preact)).astype(BF)
    pre_slopes = gather(pre_slope, "y").reshape(tokens, 2 * f)

    hiddens = jnp.concatenate([hidden, *hiddens], axis=0)
    own_slopes = jnp.concatenate([slopes[:, :d], *their_slopes], axis=0)

    def grad_of(units):
        return jnp.einsum("tf,td->fd", units, own_slopes, preferred_element_type=F32) * out_scale

    theirs = shift(grad_of(hiddens[:, f:]).astype(BF), "c", 1).astype(F32)
    grad_out = grad_of(hiddens[:, :f]) + theirs
    new_out = ema(teach_out, w_out, grad_out)

    theirs = shift((dot(gathered_t, pre_slopes[:, f:]) * in_scale).astype(BF), "c", 1).astype(F32)
    grad_in = dot(gathered_t, pre_slopes[:, :f]) * in_scale + theirs
    new_in = ema(teach_in, w_in, grad_in)
    return (grad_in.astype(BF), grad_out.astype(BF), new_in, new_out)


def solution(mesh):
    finer = Mesh(mesh.devices.reshape(2, 4, 4, 2, 2, 4), (*DP, *MP))

    def step(*args):
        return shards(*args)

    step = jax.shard_map(
        step,
        mesh=finer,
        in_specs=(P(DP, MP), P(DP, MP), P(MP, DP), P(DP, MP), P(MP, DP), P(DP, MP)),
        out_specs=(P(MP, DP), P(DP, MP), P(MP, DP), P(DP, MP)),
        check_vma=False,
    )
    return step
```

```python
import math

import jax
import jax.numpy as jnp
import numpy as np
from jax import lax
from jax.sharding import Mesh
from jax.sharding import PartitionSpec as P

D = 6144
FF = 16384
DP = ("zq", "za", "x", "c")
MP = ("zh", "y")
BF = jnp.bfloat16
F32 = jnp.float32

decay_rate = 0.99
step_size = 0.5


def exchange(pieces, axis):
    return lax.all_to_all(pieces, axis, split_axis=0, concat_axis=0, tiled=True)


def gather(value, axis):
    return exchange(jnp.broadcast_to(value, (lax.axis_size(axis), *value.shape)), axis)


def scatter(partial, axis):
    return exchange(partial.astype(BF), axis).astype(F32).sum(axis=0)


def shift(value, axis, by):
    n = lax.axis_size(axis)
    return lax.ppermute(value, axis, [(i, (i + by) % n) for i in range(n)])


def gelu_value(value):
    return 0.5 * value * (1.0 + jax.scipy.special.erf(value * (1.0 / math.sqrt(2.0))))


def gelu_slope(value):
    normal_cdf = 0.5 * (1.0 + jax.scipy.special.erf(value * (1.0 / math.sqrt(2.0))))
    return normal_cdf + value * jnp.exp(-0.5 * value * value) * (1.0 / math.sqrt(2.0 * math.pi))


def ema(teacher, student, grad):
    return decay_rate * teacher + (1.0 - decay_rate) * (student.astype(F32) - step_size * grad)


def tie(*values):
    return lax.optimization_barrier(values)


def dot(a, b):
    return jnp.dot(a, b, preferred_element_type=F32)


def shards(inputs, targets, w_in, w_out, teach_in, teach_out):
    in_scale = 1.0 / math.sqrt(D)
    out_scale = 1.0 / math.sqrt(FF)
    rows, d = inputs.shape
    f = w_in.shape[1]
    nx, na, nq, ny = (lax.axis_size(a) for a in ("x", "za", "zq", "y"))
    blocks = nx * na * nq
    tokens = blocks * rows
    part = tokens // ny
    few = rows // ny
    y = lax.axis_index("y")

    w_both = shift(w_in, "c", 1)
    w_ring = [w_out, shift(w_out, "y", -1), None, shift(w_out, "y", 1)]
    near = gather(inputs, ("za", "zq"))
    near, w_later = tie(near, w_out)
    w_ring[2] = shift(w_later, "y", 2)
    w_both = jnp.concatenate([w_in, w_both], axis=1)

    at = np.arange(na * nq * rows)
    source = at % (part // nx) // few * rows + at // (part // nx) * few + at % few
    order = jnp.asarray(np.eye(at.size, dtype=np.float32)[source], BF)
    near = dot(order, near.reshape(at.size, d)).astype(BF)

    arrived = gather(near, "x")
    arrived, w_both, w_ring[1], w_ring[3] = tie(arrived, w_both, w_ring[1], w_ring[3])
    w_ring = jnp.concatenate(w_ring, axis=1)

    partial_pre = (dot(arrived.reshape(tokens, d), w_both) * in_scale).astype(BF)
    partial_pre = partial_pre.reshape(nx, ny, part // nx, 2 * f).swapaxes(0, 1)
    sums = scatter(partial_pre.reshape(ny, part, 2 * f), "y")

    sums, w_ring = tie(sums, w_ring)
    other = shift(sums.astype(BF), "zh", 1)
    w_ring_theirs = shift(w_ring, "c", 1)

    both = jnp.stack([inputs.reshape(ny, few, d), targets.reshape(ny, few, d)], axis=1)
    both = exchange(both, "y")
    both = both.astype(F32)
    own = both[:, 0] - both[:, 1]
    own = jnp.concatenate(
        [lax.dynamic_index_in_dim(own, (y + k) & (ny - 1), keepdims=False) for k in range(ny)],
        axis=1,
    )
    own, other = tie(own, other)
    preact = sums + other.astype(F32)
    hidden = gelu_value(preact).astype(BF)
    hiddens = []
    for k in range(1, ny):
        hiddens.append(shift(hidden, "y", k))

    partial_out = (dot(hidden[:, :f], w_ring) + dot(hidden[:, f:], w_ring_theirs)) * out_scale
    partial_out, arrived = tie(partial_out, arrived)
    sums = scatter(partial_out.reshape(nx, part // nx, ny * d), "x")
    gathered_t = arrived.reshape(nx, ny, part // nx, d).swapaxes(0, 1).reshape(tokens, d).T
    sums, gathered_t = tie(sums, gathered_t)
    sums = scatter(sums.reshape(na, nq * few, ny * d), "za")
    mine = lax.broadcasted_iota(jnp.int32, (nq * few, 1), 0) // few == lax.axis_index("zq")
    sums = sums + jnp.where(mine, jnp.concatenate([own] * nq, axis=0), 0.0)
    other = shift(sums.astype(BF), "zq", 1)
    slope = (sums + other.astype(F32)).astype(BF)
    slopes = gather(slope, "za")
    slopes = gather(slopes, "x")
    slopes = slopes.reshape(part, ny * d)

    slope_part = out_scale * jnp.concatenate(
        [
            jnp.einsum("td,fd->tf", slopes, w, preferred_element_type=F32)
            for w in (w_ring, w_ring_theirs)
        ],
        axis=1,
    )
    slopes, slope_part = tie(slopes, slope_part)
    other = shift(slope_part.astype(BF), "zh", 1)
    their_slopes = [shift(slopes[:, k * d : (k + 1) * d], "y", k) for k in range(1, ny)]
    hidden_slope = slope_part + other.astype(F32)
    pre_slope = (hidden_slope * gelu_slope(preact)).astype(BF)
    pre_slopes = gather(pre_slope, "y")
    pre_slopes = pre_slopes.reshape(tokens, 2 * f)

    hiddens = jnp.concatenate([hidden, *hiddens], axis=0)
    own_slopes = jnp.concatenate([slopes[:, :d], *their_slopes], axis=0)

    def grad_of(units):
        return jnp.einsum("tf,td->fd", units, own_slopes, preferred_element_type=F32) * out_scale

    theirs = shift(grad_of(hiddens[:, f:]).astype(BF), "c", 1).astype(F32)
    grad_out = grad_of(hiddens[:, :f]) + theirs
    new_out = ema(teach_out, w_out, grad_out)

    theirs = shift((dot(gathered_t, pre_slopes[:, f:]) * in_scale).astype(BF), "c", 1).astype(F32)
    grad_in = dot(gathered_t, pre_slopes[:, :f]) * in_scale + theirs
    new_in = ema(teach_in, w_in, grad_in)
    return (grad_in.astype(BF), grad_out.astype(BF), new_in, new_out)


def solution(mesh):
    finer = Mesh(mesh.devices.reshape(2, 4, 4, 2, 2, 4), (*DP, *MP))

    def step(*args):
        return shards(*args)

    step = jax.shard_map(
        step,
        mesh=finer,
        in_specs=(P(DP, MP), P(DP, MP), P(MP, DP), P(DP, MP), P(MP, DP), P(DP, MP)),
        out_specs=(P(MP, DP), P(DP, MP), P(MP, DP), P(DP, MP)),
        check_vma=False,
    )
    return step
```

```python
import math

import jax
import jax.numpy as jnp
import numpy as np
from jax import lax
from jax.experimental.layout import Layout, with_layout_constraint
from jax.sharding import Mesh
from jax.sharding import PartitionSpec as P

D = 6144
FF = 16384
DP = ("zq", "za", "x", "c")
MP = ("zh", "y")
BF = jnp.bfloat16
F32 = jnp.float32


decay_rate = 0.99
step_size = 0.5


def exchange(pieces, axis):
    return lax.all_to_all(pieces, axis, split_axis=0, concat_axis=0, tiled=True)


def gather(value, axis):
    return exchange(jnp.broadcast_to(value, (lax.axis_size(axis), *value.shape)), axis)


def scatter(partial, axis):
    return exchange(partial.astype(BF), axis).astype(F32).sum(axis=0)


def shift(value, axis, by):
    n = lax.axis_size(axis)
    return lax.ppermute(value, axis, [(i, (i + by) % n) for i in range(n)])


def gelu_value(value):
    return 0.5 * value * (1.0 + jax.scipy.special.erf(value * (1.0 / math.sqrt(2.0))))


def gelu_slope(value):
    normal_cdf = 0.5 * (1.0 + jax.scipy.special.erf(value * (1.0 / math.sqrt(2.0))))
    return normal_cdf + value * jnp.exp(-0.5 * value * value) * (1.0 / math.sqrt(2.0 * math.pi))


def ema(teacher, student, grad):
    return decay_rate * teacher + (1.0 - decay_rate) * (student.astype(F32) - step_size * grad)


def tie(*values):
    return lax.optimization_barrier(values)


def dot(a, b):
    return jnp.dot(a, b, preferred_element_type=F32)


def shards(inputs, targets, w_in, w_out, teach_in, teach_out):
    in_scale = 1.0 / math.sqrt(D)
    out_scale = 1.0 / math.sqrt(FF)
    rows, d = inputs.shape
    f = w_in.shape[1]
    nx, na, nq, ny = (lax.axis_size(a) for a in ("x", "za", "zq", "y"))
    blocks = nx * na * nq
    tokens = blocks * rows
    part = tokens // ny
    few = rows // ny
    y = lax.axis_index("y")

    w_both = shift(w_in, "c", 1)
    w_ring = [w_out, shift(w_out, "y", -1), None, shift(w_out, "y", 1)]
    near = gather(inputs, ("za", "zq"))
    near, w_later = tie(near, w_out)
    w_ring[2] = shift(w_later, "y", 2)
    w_both = jnp.concatenate([w_in, w_both], axis=1)

    at = np.arange(na * nq * rows)
    source = at % (part // nx) // few * rows + at // (part // nx) * few + at % few
    order = jnp.asarray(np.eye(at.size, dtype=np.float32)[source], BF)
    near = dot(order, near.reshape(at.size, d)).astype(BF)
    near = with_layout_constraint(near, Layout((0, 1)))

    arrived = gather(near, "x")
    arrived, w_both, w_ring[1], w_ring[3] = tie(arrived, w_both, w_ring[1], w_ring[3])
    w_ring = jnp.concatenate(w_ring, axis=1)

    partial_pre = (dot(arrived.reshape(tokens, d), w_both) * in_scale).astype(BF)
    partial_pre = partial_pre.reshape(nx, ny, part // nx, 2 * f).swapaxes(0, 1)
    sums = scatter(partial_pre.reshape(ny, part, 2 * f), "y")

    sums, w_ring = tie(sums, w_ring)
    other = shift(sums.astype(BF), "zh", 1)
    w_ring_theirs = shift(w_ring, "c", 1)

    both = jnp.stack([inputs.reshape(ny, few, d), targets.reshape(ny, few, d)], axis=1)
    both = exchange(both, "y")
    both = both.astype(F32)
    own = both[:, 0] - both[:, 1]
    own = jnp.concatenate(
        [lax.dynamic_index_in_dim(own, (y + k) & (ny - 1), keepdims=False) for k in range(ny)],
        axis=1,
    )
    mine = lax.broadcasted_iota(jnp.int32, (nq * few, 1), 0) // few == lax.axis_index("zq")
    own = jnp.where(mine, jnp.concatenate([own] * nq, axis=0), 0.0)
    first = lax.axis_index("c") == 0
    own, other, first = tie(own, other, first)
    preact = sums + other.astype(F32)
    hidden = gelu_value(preact).astype(BF)
    hiddens = []
    for k in range(1, ny):
        hiddens.append(shift(hidden, "y", k))

    partial_out = (dot(hidden[:, :f], w_ring) + dot(hidden[:, f:], w_ring_theirs)) * out_scale
    partial_out, arrived = tie(partial_out, arrived)
    sums = scatter(partial_out.reshape(nx, part // nx, ny * d), "x")
    gathered_t = arrived.reshape(nx, ny, part // nx, d).swapaxes(0, 1).reshape(tokens, d).T
    gathered_t = with_layout_constraint(gathered_t, Layout((0, 1)))
    sums, gathered_t = tie(sums, gathered_t)
    sums = scatter(sums.reshape(na, nq * few, ny * d), "za")
    sums = sums + own
    other = shift(sums.astype(BF), "zq", 1)
    turned = shift(gathered_t, "c", 1)
    slope = (sums + other.astype(F32)).astype(BF)
    slopes = gather(slope, "za")
    slopes = gather(slopes, "x")
    slopes = slopes.reshape(part, ny * d)

    slope_part = out_scale * jnp.concatenate(
        [
            jnp.einsum("td,fd->tf", slopes, w, preferred_element_type=F32)
            for w in (w_ring, w_ring_theirs)
        ],
        axis=1,
    )
    slopes, slope_part = tie(slopes, slope_part)
    other = shift(slope_part.astype(BF), "zh", 1)
    their_slopes = [shift(slopes[:, k * d : (k + 1) * d], "y", k) for k in range(1, ny)]
    turned = jnp.concatenate(
        [jnp.where(first, gathered_t, turned), jnp.where(first, turned, gathered_t)], axis=1
    )
    other, turned = tie(other, turned)
    pre_slope = ((slope_part + other.astype(F32)) * gelu_slope(preact)).astype(BF)
    halves = pre_slope[:, :f], pre_slope[:, f:]
    halves = jnp.stack([jnp.where(first, *halves), jnp.where(first, *halves[::-1])])
    halves = jnp.broadcast_to(halves[:, None], (2, ny, part, f)).reshape(2 * ny, part, f)
    pre_slopes = exchange(halves, ("c", "y")).reshape(2 * tokens, f)

    hiddens = jnp.concatenate([hidden, *hiddens], axis=0)
    own_slopes = jnp.concatenate([slopes[:, :d], *their_slopes], axis=0)

    def grad_of(units):
        return jnp.einsum("tf,td->fd", units, own_slopes, preferred_element_type=F32) * out_scale

    theirs = grad_of(hiddens[:, f:]).astype(BF)
    theirs = shift(theirs, "c", 1).astype(F32)
    grad_out = grad_of(hiddens[:, :f]) + theirs
    new_out = ema(teach_out, w_out, grad_out)

    grad_in = dot(turned, pre_slopes) * in_scale
    new_in = ema(teach_in, w_in, grad_in)
    return (grad_in.astype(BF), grad_out.astype(BF), new_in, new_out)


def solution(mesh):
    finer = Mesh(mesh.devices.reshape(2, 4, 4, 2, 2, 4), (*DP, *MP))

    def step(*args):
        return shards(*args)

    step = jax.shard_map(
        step,
        mesh=finer,
        in_specs=(P(DP, MP), P(DP, MP), P(MP, DP), P(DP, MP), P(MP, DP), P(DP, MP)),
        out_specs=(P(MP, DP), P(DP, MP), P(MP, DP), P(DP, MP)),
        check_vma=False,
    )
    return step
```

```python
import math

import jax
import jax.numpy as jnp
import numpy as np
from jax import lax
from jax.experimental.layout import Layout, with_layout_constraint
from jax.sharding import Mesh
from jax.sharding import PartitionSpec as P

D = 6144
FF = 16384
DP = ("zq", "za", "x", "c")
MP = ("zh", "y")
BF = jnp.bfloat16
F32 = jnp.float32


decay_rate = 0.99
step_size = 0.5


def exchange(pieces, axis):
    return lax.all_to_all(pieces, axis, split_axis=0, concat_axis=0, tiled=True)


def gather(value, axis):
    return exchange(jnp.broadcast_to(value, (lax.axis_size(axis), *value.shape)), axis)


def scatter(partial, axis):
    return exchange(partial.astype(BF), axis).astype(F32).sum(axis=0)


def shift(value, axis, by):
    n = lax.axis_size(axis)
    return lax.ppermute(value, axis, [(i, (i + by) % n) for i in range(n)])


def gelu_value(value):
    return 0.5 * value * (1.0 + jax.scipy.special.erf(value * (1.0 / math.sqrt(2.0))))


def gelu_slope(value):
    normal_cdf = 0.5 * (1.0 + jax.scipy.special.erf(value * (1.0 / math.sqrt(2.0))))
    return normal_cdf + value * jnp.exp(-0.5 * value * value) * (1.0 / math.sqrt(2.0 * math.pi))


def ema(teacher, student, grad):
    return decay_rate * teacher + (1.0 - decay_rate) * (student.astype(F32) - step_size * grad)


def tie(*values):
    return lax.optimization_barrier(values)


def dot(a, b):
    return jnp.dot(a, b, preferred_element_type=F32)


def shards(inputs, targets, w_in, w_out, teach_in, teach_out):
    in_scale = 1.0 / math.sqrt(D)
    out_scale = 1.0 / math.sqrt(FF)
    rows, d = inputs.shape
    f = w_in.shape[1]
    nx, na, nq, ny = (lax.axis_size(a) for a in ("x", "za", "zq", "y"))
    blocks = nx * na * nq
    tokens = blocks * rows
    part = tokens // ny
    few = rows // ny
    y = lax.axis_index("y")

    w_both = shift(w_in, "c", 1)
    w_ring = [w_out, shift(w_out, "y", -1), None, shift(w_out, "y", 1)]
    near = gather(inputs, ("za", "zq"))
    near, w_later = tie(near, w_out)
    w_ring[2] = shift(w_later, "y", 2)
    w_both = jnp.concatenate([w_in, w_both], axis=1)

    at = np.arange(na * nq * rows)
    source = at % (part // nx) // few * rows + at // (part // nx) * few + at % few
    order = jnp.asarray(np.eye(at.size, dtype=np.float32)[source], BF)
    near = dot(order, near.reshape(at.size, d)).astype(BF)
    near = with_layout_constraint(near, Layout((0, 1)))

    arrived = gather(near, "x")
    arrived, w_both, w_ring[1], w_ring[3] = tie(arrived, w_both, w_ring[1], w_ring[3])
    w_ring = jnp.concatenate(w_ring, axis=1)

    partial_pre = (dot(arrived.reshape(tokens, d), w_both) * in_scale).astype(BF)
    partial_pre = partial_pre.reshape(nx, ny, part // nx, 2 * f).swapaxes(0, 1)
    sums = scatter(partial_pre.reshape(ny, part, 2 * f), "y")
    gathered_t = arrived.reshape(nx, ny, part // nx, d).swapaxes(0, 1).reshape(tokens, d).T
    gathered_t = with_layout_constraint(gathered_t, Layout((0, 1)))

    sums, w_ring, gathered_t = tie(sums, w_ring, gathered_t)
    other = shift(sums.astype(BF), "zh", 1)
    w_ring_theirs = shift(w_ring, "c", 1)

    both = jnp.stack([inputs.reshape(ny, few, d), targets.reshape(ny, few, d)], axis=1)
    both = exchange(both, "y")
    both = both.astype(F32)
    own = both[:, 0] - both[:, 1]
    own = jnp.concatenate(
        [lax.dynamic_index_in_dim(own, (y + k) & (ny - 1), keepdims=False) for k in range(ny)],
        axis=1,
    )
    mine = lax.broadcasted_iota(jnp.int32, (nq * few, 1), 0) // few == lax.axis_index("zq")
    own = jnp.where(mine, jnp.concatenate([own] * nq, axis=0), 0.0)
    first = lax.axis_index("c") == 0
    own, other, first = tie(own, other, first)
    preact = sums + other.astype(F32)
    hidden = gelu_value(preact).astype(BF)
    hiddens = []
    for k in range(1, ny):
        hiddens.append(shift(hidden, "y", k))

    partial_out = (dot(hidden[:, :f], w_ring) + dot(hidden[:, f:], w_ring_theirs)) * out_scale
    sums = scatter(partial_out.reshape(nx, part // nx, ny * d), "x")
    sums = scatter(sums.reshape(na, nq * few, ny * d), "za")
    sums = sums + own
    other = shift(sums.astype(BF), "zq", 1)
    turned = shift(gathered_t, "c", 1)
    slope = (sums + other.astype(F32)).astype(BF)
    slopes = gather(slope, "za")
    slopes = lax.all_gather(slopes, "x")
    slopes = slopes.reshape(part, ny * d)

    slope_part = out_scale * jnp.concatenate(
        [
            jnp.einsum("td,fd->tf", slopes, w, preferred_element_type=F32)
            for w in (w_ring, w_ring_theirs)
        ],
        axis=1,
    )
    slopes, slope_part = tie(slopes, slope_part)
    other = shift(slope_part.astype(BF), "zh", 1)
    their_slopes = [shift(slopes[:, k * d : (k + 1) * d], "y", k) for k in range(1, ny)]
    turned = jnp.concatenate(
        [jnp.where(first, gathered_t, turned), jnp.where(first, turned, gathered_t)], axis=1
    )
    other, turned = tie(other, turned)
    pre_slope = ((slope_part + other.astype(F32)) * gelu_slope(preact)).astype(BF)
    halves = pre_slope[:, :f], pre_slope[:, f:]
    halves = jnp.stack([jnp.where(first, *halves), jnp.where(first, *halves[::-1])])
    halves = jnp.broadcast_to(halves[:, None], (2, ny, part, f)).reshape(2 * ny, part, f)
    pre_slopes = exchange(halves, ("c", "y")).reshape(2 * tokens, f)

    hiddens = jnp.concatenate([hidden, *hiddens], axis=0)
    own_slopes = jnp.concatenate([slopes[:, :d], *their_slopes], axis=0)

    def grad_of(units):
        return jnp.einsum("tf,td->fd", units, own_slopes, preferred_element_type=F32) * out_scale

    theirs = grad_of(hiddens[:, f:]).astype(BF)
    theirs = shift(theirs, "c", 1).astype(F32)
    theirs, ours = tie(theirs, grad_of(hiddens[:, :f]))
    grad_out = ours + theirs
    new_out = ema(teach_out, w_out, grad_out)

    grad_in = dot(turned, pre_slopes) * in_scale
    new_in = ema(teach_in, w_in, grad_in)
    return (grad_in.astype(BF), grad_out.astype(BF), new_in, new_out)


def solution(mesh):
    finer = Mesh(mesh.devices.reshape(2, 4, 4, 2, 2, 4), (*DP, *MP))

    def step(*args):
        return shards(*args)

    step = jax.shard_map(
        step,
        mesh=finer,
        in_specs=(P(DP, MP), P(DP, MP), P(MP, DP), P(DP, MP), P(MP, DP), P(DP, MP)),
        out_specs=(P(MP, DP), P(DP, MP), P(MP, DP), P(DP, MP)),
        check_vma=False,
    )
    return step
```
